32 devices in a mesh: row: 4 (over z), col: 8 (over y, x, core).
Axes of the slice: x: 2, y: 2, z: 4, core: 2. Of those that a mesh axis runs over, the one named last changes fastest.
Arguments:
- b_tensor: bfloat16 [128, 512, 512], P('col', 'row'), may hold values from -0.4 to 0.4, as said below
- ri_pairs: int32 [128, 4, 4], P('col'), may hold values from 0 to 1, as said below
- g_occ: bfloat16 [512, 512], P(None, 'col'), may hold values from -0.25 to 0.25
- g_vir: bfloat16 [512, 512], P(None, 'col'), may hold values from -0.25 to 0.25
- occ_mask: int32 [4, 4], replicated, may hold values 0 or 1
- vir_mask: int32 [4, 4], replicated, may hold values 0 or 1
Outputs:
- chi: float32 [128, 128], P('col', 'row')
The draws below stay inside these ranges and needn't reach their ends.
Inputs may be any that keep to these rules, and one draw needn't show every extreme that they name: b_tensor[p] is a symmetric matrix for every p. ri_pairs[p] is symmetric with ones on its diagonal.
All inputs are finite; a program needn't handle non-finite values.
Results may differ from the reference program's by a relative error of at most 0.004.
Values may be sent and summed in bfloat16 or wider, within the bound.
A program may use at most 64 MiB of HBM per device.

```python
import jax
import jax.numpy as jnp
from jax import lax

BS = 128
NA = 4
NAO = 512
NRI = 128


def draw_b_tensor(key, part):
    first_key = jax.random.fold_in(key, 11)
    base_values = jax.random.truncated_normal(first_key, -4.0, 4.0, (NRI, NAO, NAO), jnp.float32)
    return ((base_values + jnp.swapaxes(base_values, 1, 2)) * 0.0283).astype(jnp.bfloat16)


def draw_ri_pairs(key, part):
    upper_bits = jax.random.randint(jax.random.fold_in(key, 21), (NRI, NA, NA), 0, 2, dtype=jnp.int32)
    row_ids = lax.broadcasted_iota(jnp.int32, (NA, NA), 0)
    col_ids = lax.broadcasted_iota(jnp.int32, (NA, NA), 1)
    symmetric = jnp.where(row_ids < col_ids, upper_bits, jnp.swapaxes(upper_bits, 1, 2))
    return jnp.where(row_ids == col_ids, 1, symmetric).astype(jnp.int32)


def with_ends(array, key, low, high):
    extent = array.shape
    place = [jax.random.randint(jax.random.fold_in(key, axis), (), 0, extent[axis]) for axis in range(len(extent))]
    array = array.at[tuple(place)].set(low)
    longest = extent.index(max(extent))
    place[longest] = (place[longest] + 1) % extent[longest]
    return array.at[tuple(place)].set(high)


def steps_of(key, shape, cuts, low, top_value):
    factor_of = 1.0
    for dim, parts in cuts:
        steps = jax.random.uniform(jax.random.fold_in(jax.random.fold_in(key, 6), dim), (parts,), jnp.float32, low / len(cuts), top_value / len(cuts))
        factor_of = factor_of * jnp.repeat(jnp.exp(steps), shape[dim] // parts).reshape((-1,) + (1,) * (len(shape) - 1 - dim))
    return factor_of


def noise(own_key, dims, deviation, most, shards=(), kind=jnp.bfloat16):
    result = jax.random.normal(own_key, dims, jnp.float32) * deviation
    if len(shards) > 0:
        result = steps_of(own_key, dims, shards, -0.22, 0.18) * result
    return jnp.clip(result, min=-most, max=most).astype(kind)


def setup_inputs(seed: int = 0) -> dict:
    key_list = jax.random.split(jax.random.key(seed), 7)
    b_tensor = draw_b_tensor(jax.random.fold_in(key_list[6], 71), 0)
    ri_pairs = draw_ri_pairs(jax.random.fold_in(key_list[6], 71), 0)
    g_occ = noise(key_list[2], (NAO, NAO), NAO ** -0.5, 0.25, ((1, 8),))
    g_vir = noise(key_list[3], (NAO, NAO), NAO ** -0.5, 0.25, ((1, 8),))
    occ_mask = with_ends((jax.random.randint(key_list[4], (NA, NA), 0, 2) < 1).astype(jnp.int32), jax.random.fold_in(key_list[4], 1), 0, 1)
    vir_mask = with_ends((jax.random.randint(key_list[5], (NA, NA), 0, 2) < 1).astype(jnp.int32), jax.random.fold_in(key_list[5], 1), 0, 1)
    return dict(b_tensor=b_tensor, ri_pairs=ri_pairs, g_occ=g_occ, g_vir=g_vir, occ_mask=occ_mask, vir_mask=vir_mask)


def spread(mask):
    return jnp.repeat(jnp.repeat(mask, BS, axis=-2), BS, axis=-1)


def reference(b_tensor, ri_pairs, g_occ, g_vir, occ_mask, vir_mask):
    occ_green = (g_occ * spread(occ_mask).astype(jnp.bfloat16)).astype(jnp.float32)
    vir_green = (g_vir * spread(vir_mask).astype(jnp.bfloat16)).astype(jnp.float32)

    def one_function(pieces):
        integral, pattern = pieces
        masked = (integral * spread(pattern).astype(jnp.bfloat16)).astype(jnp.float32)
        occ_side = jnp.dot(occ_green, masked, precision=lax.Precision.HIGHEST)
        vir_side = jnp.dot(masked, vir_green, precision=lax.Precision.HIGHEST)
        return occ_side.astype(jnp.bfloat16), vir_side.astype(jnp.bfloat16)

    occ_side, vir_side = lax.map(one_function, (b_tensor, ri_pairs))

    def add_block(total, index):
        occ_rows = lax.dynamic_slice_in_dim(occ_side, index * BS, BS, 1).reshape(NRI, BS * NAO).astype(jnp.float32)
        vir_rows = lax.dynamic_slice_in_dim(vir_side, index * BS, BS, 1).reshape(NRI, BS * NAO).astype(jnp.float32)
        return total + jnp.dot(occ_rows, vir_rows.T, precision=lax.Precision.HIGHEST), None

    chi, _ = lax.scan(add_block, jnp.zeros((NRI, NRI), jnp.float32), jnp.arange(NA, dtype=jnp.int32))
    return chi
```

```python
import functools

import jax
import jax.numpy as jnp
from jax import lax
from jax.experimental import pallas as pl
from jax.experimental.pallas import tpu as pltpu
from jax.sharding import PartitionSpec as P

BS = 128


def kernel(nr, nc, ri_ref, om_ref, vm_ref, b_ref, go_ref, gv_ref, out_ref,
           gv_slots, go_slots, gv, go, wide, v16, o16, vir_all, occ_all,
           chi, red1, st2, red2,
           g_send, g_recv, v_send, v_recv, o_send, o_recv,
           r1_send, r1_recv, r2_send, r2_recv):
    r = lax.axis_index("row")
    c = lax.axis_index("col")
    me = r * nc + c
    n_dev = nr * nc
    np_, rows, n = b_ref.shape
    na = n // BS
    pc = rows // nc
    packed = gv_ref.shape[0]
    q = n // packed
    w = n // nc

    def remote(src, dst, send, recv, row, col):
        return pltpu.make_async_remote_copy(
            src_ref=src, dst_ref=dst, send_sem=send, recv_sem=recv,
            device_id={"row": row, "col": col}, device_id_type=pl.DeviceIdType.MESH)

    barrier = pltpu.get_barrier_semaphore()

    def greet(i, _):
        t = lax.rem(me + i, n_dev)
        pl.semaphore_signal(barrier, inc=1,
                            device_id={"row": t // nc, "col": lax.rem(t, nc)},
                            device_id_type=pl.DeviceIdType.MESH)
        return 0

    lax.fori_loop(1, n_dev, greet, 0)
    pl.semaphore_wait(barrier, n_dev - 1)

    def g_copy(i, kind):
        t = lax.rem(c + i, nc)
        src, dst = (gv_ref, gv_slots) if kind == 0 else (go_ref, go_slots)
        return remote(src, dst.at[c], g_send.at[kind, i], g_recv.at[kind, i], r, t)

    for kind in (0, 1):
        def g_start(i, _):
            g_copy(i, kind).start()
            return 0
        lax.fori_loop(1, nc, g_start, 0)
    gv_slots[pl.ds(c, 1)] = gv_ref[...][None]
    go_slots[pl.ds(c, 1)] = go_ref[...][None]

    def assemble(kind, slots, full, mask):
        def g_wait(i, _):
            g_copy(i, kind).wait_recv()
            return 0
        lax.fori_loop(1, nc, g_wait, 0)
        per = BS // w
        for i in range(q):
            for j in range(na):
                block = jnp.concatenate(
                    [slots[j * per + k][:, i * w:(i + 1) * w] for k in range(per)], axis=1)
                for h in range(packed // BS):
                    m = mask[(i * packed // BS + h) * na + j].astype(jnp.float32)
                    piece = block[h * BS:(h + 1) * BS].astype(jnp.float32) * m
                    full[i * packed + h * BS:i * packed + (h + 1) * BS,
                         j * BS:(j + 1) * BS] = piece.astype(jnp.bfloat16)

    assemble(0, gv_slots, gv, vm_ref)

    def round_rows(dst):
        def one(i, _):
            for s in range(nr):
                dst[s, pl.ds(i * pc, pc)] = wide[s, pl.ds(i * pc, pc)].astype(jnp.bfloat16)
            return 0
        lax.fori_loop(0, nc, one, 0)

    for p in range(np_):
        row = jnp.concatenate(
            [jnp.full((1, BS), ri_ref[(p * na + r) * na + j].astype(jnp.float32)) for j in range(na)],
            axis=1)
        bm = (b_ref[p].astype(jnp.float32) * row).astype(jnp.bfloat16)

        res = jnp.dot(bm, gv[...], preferred_element_type=jnp.float32)
        for s in range(nr):
            wide[s, :, p, :] = res[:, s * BS:(s + 1) * BS]
    round_rows(v16)

    def v_copy(i):
        t = lax.rem(me + i, n_dev)
        tr, tc = t // nc, lax.rem(t, nc)
        return remote(v16.at[tr, pl.ds(tc * pc, pc)], vir_all.at[r, :, c],
                      v_send.at[i], v_recv.at[r, c], tr, tc)

    def v_start(i, _):
        v_copy(i).start()
        return 0

    lax.fori_loop(1, n_dev, v_start, 0)
    vir_all[pl.ds(r, 1), :, pl.ds(c, 1)] = v16[pl.ds(r, 1), pl.ds(c * pc, pc)][:, :, None]

    assemble(1, go_slots, go, om_ref)
    for p in range(np_):
        row = jnp.concatenate(
            [jnp.full((1, BS), ri_ref[(p * na + r) * na + j].astype(jnp.float32)) for j in range(na)],
            axis=1)
        bm = (b_ref[p].astype(jnp.float32) * row).astype(jnp.bfloat16)
        res = lax.dot_general(go[...], bm, (((1,), (1,)), ((), ())),
                              preferred_element_type=jnp.float32)
        for s in range(nr):
            wide[s, :, p, :] = res[s * BS:(s + 1) * BS]
    round_rows(o16)

    def o_copy(i):
        t = lax.rem(c + i, nc)
        return remote(o16.at[:, pl.ds(t * pc, pc)], occ_all.at[:, :, c],
                      o_send.at[i], o_recv.at[i], r, t)

    def o_start(i, _):
        o_copy(i).start()
        return 0

    lax.fori_loop(1, nc, o_start, 0)
    occ_all[:, :, pl.ds(c, 1)] = o16[:, pl.ds(c * pc, pc)][:, :, None]

    def o_wait(i, _):
        o_copy(i).wait_recv()
        return 0

    lax.fori_loop(1, nc, o_wait, 0)

    total_ri = nc * np_
    chi[...] = jnp.zeros_like(chi)
    step = min(pc, 8)
    for off in range(nr):
        rr = lax.rem(r + off, nr)

        def v_wait(j, _):
            col = lax.rem(c + j, nc)
            remote(v16.at[0, pl.ds(0, pc)], vir_all.at[rr, :, col],
                   v_send.at[0], v_recv.at[rr, col], rr, col).wait_recv()
            return 0

        lax.fori_loop(1 if off == 0 else 0, nc, v_wait, 0)
        for k in range(0, pc, step):
            left = occ_all[rr, k:k + step].reshape(step, total_ri, BS)
            right = vir_all[rr, k:k + step].reshape(step, total_ri, BS)
            left = jnp.concatenate([left[i] for i in range(step)], axis=1)
            right = jnp.concatenate([right[i] for i in range(step)], axis=1)
            chi[...] += lax.dot_general(
                left, right, (((1,), (1,)), ((), ())),
                preferred_element_type=jnp.float32).reshape(nc, np_, total_ri)

    def r1_copy(i):
        t = lax.rem(c + i, nc)
        return remote(chi.at[t], red1.at[c], r1_send.at[i], r1_recv.at[i], r, t)

    def r1_start(i, _):
        r1_copy(i).start()
        return 0

    lax.fori_loop(1, nc, r1_start, 0)
    red1[pl.ds(c, 1)] = chi[pl.ds(c, 1)]

    def r1_wait(i, _):
        r1_copy(i).wait_recv()
        return 0

    lax.fori_loop(1, nc, r1_wait, 0)
    part = red1[0]
    for k in range(1, nc):
        part = part + red1[k]
    wc = total_ri // nr
    for s in range(nr):
        st2[s] = part[:, s * wc:(s + 1) * wc]

    def r2_copy(i):
        t = lax.rem(r + i, nr)
        return remote(st2.at[t], red2.at[r], r2_send.at[i], r2_recv.at[i], t, c)

    for i in range(1, nr):
        r2_copy(i).start()
    red2[pl.ds(r, 1)] = st2[pl.ds(r, 1)]
    for i in range(1, nr):
        r2_copy(i).wait_recv()
    acc = red2[0]
    for k in range(1, nr):
        acc = acc + red2[k]
    out_ref[...] = acc

    for kind in (0, 1):
        def g_sent(i, _):
            g_copy(i, kind).wait_send()
            return 0
        lax.fori_loop(1, nc, g_sent, 0)

    def v_sent(i, _):
        v_copy(i).wait_send()
        return 0

    lax.fori_loop(1, n_dev, v_sent, 0)

    def col_sent(i, _):
        o_copy(i).wait_send()
        r1_copy(i).wait_send()
        return 0

    lax.fori_loop(1, nc, col_sent, 0)
    for i in range(1, nr):
        r2_copy(i).wait_send()


def body(nr, nc, b_tensor, ri_pairs, g_occ, g_vir, occ_mask, vir_mask):
    np_, rows, n = b_tensor.shape
    w = n // nc
    q = BS // w
    pc = rows // nc
    total_ri = nc * np_

    def pack(g):
        return jnp.concatenate([g[i * (n // q):(i + 1) * (n // q)] for i in range(q)], axis=1)

    vmem = pl.BlockSpec(memory_space=pltpu.VMEM)
    smem = pl.BlockSpec(memory_space=pltpu.SMEM)
    bf16, f32 = jnp.bfloat16, jnp.float32
    dma = pltpu.SemaphoreType.DMA
    return pl.pallas_call(
        functools.partial(kernel, nr, nc),
        out_shape=jax.ShapeDtypeStruct((np_, total_ri // nr), f32),
        in_specs=[smem, smem, smem, vmem, vmem, vmem],
        out_specs=vmem,
        scratch_shapes=[
            pltpu.VMEM((nc, n // q, BS), bf16),
            pltpu.VMEM((nc, n // q, BS), bf16),
            pltpu.VMEM((n, n), bf16),
            pltpu.VMEM((n, n), bf16),
            pltpu.VMEM((nr, rows, np_, BS), f32),
            pltpu.VMEM((nr, rows, np_, BS), bf16),
            pltpu.VMEM((nr, rows, np_, BS), bf16),
            pltpu.VMEM((nr, pc, nc, np_, BS), bf16),
            pltpu.VMEM((nr, pc, nc, np_, BS), bf16),
            pltpu.VMEM((nc, np_, total_ri), f32),
            pltpu.VMEM((nc, np_, total_ri), f32),
            pltpu.VMEM((nr, np_, total_ri // nr), f32),
            pltpu.VMEM((nr, np_, total_ri // nr), f32),
            dma((2, nc)), dma((2, nc)),
            dma((nr * nc,)), dma((nr, nc)),
            dma((nc,)), dma((nc,)),
            dma((nc,)), dma((nc,)),
            dma((nr,)), dma((nr,)),
        ],
        compiler_params=pltpu.CompilerParams(
            collective_id=0, has_side_effects=True, vmem_limit_bytes=56 * 1024 * 1024),
    )(ri_pairs.reshape(-1), occ_mask.reshape(-1), vir_mask.reshape(-1), b_tensor, pack(g_occ), pack(g_vir))


def solution(mesh):
    in_specs = (
        P("col", "row", None),
        P("col", None, None),
        P(None, "col"),
        P(None, "col"),
        P(),
        P(),
    )
    return jax.shard_map(
        functools.partial(body, mesh.shape["row"], mesh.shape["col"]),
        mesh=mesh, in_specs=in_specs, out_specs=P("col", "row"), check_vma=False)
```

```python
import functools

import jax
import jax.numpy as jnp
from jax import lax
from jax.experimental import pallas as pl
from jax.experimental.pallas import tpu as pltpu
from jax.sharding import PartitionSpec as P

BS = 128


def kernel(nr, nc, ri_ref, om_ref, vm_ref, b_hbm, go_ref, gv_ref, out_ref,
           b_ref, gv_slots, go_slots, gv, go, wide, v16, o16, vir_all, occ_all,
           chi, red1, st2, red2,
           b_sem, g_send, g_recv, v_send, v_recv, o_send, o_recv,
           r1_send, r1_recv, r2_send, r2_recv):
    r = lax.axis_index("row")
    c = lax.axis_index("col")
    me = r * nc + c
    n_dev = nr * nc
    np_, rows, n = b_ref.shape
    na = n // BS
    pc = rows // nc
    w = n // nc

    def remote(src, dst, send, recv, row, col):
        return pltpu.make_async_remote_copy(
            src_ref=src, dst_ref=dst, send_sem=send, recv_sem=recv,
            device_id={"row": row, "col": col}, device_id_type=pl.DeviceIdType.MESH)

    fetch = pltpu.make_async_copy(b_hbm, b_ref, b_sem)
    fetch.start()
    barrier = pltpu.get_barrier_semaphore()

    def greet(i, _):
        t = lax.rem(me + i, n_dev)
        pl.semaphore_signal(barrier, inc=1,
                            device_id={"row": t // nc, "col": lax.rem(t, nc)},
                            device_id_type=pl.DeviceIdType.MESH)
        return 0

    lax.fori_loop(1, n_dev, greet, 0)
    for src, slots in ((gv_ref, gv_slots), (go_ref, go_slots)):
        slots[pl.ds(c, 1)] = src[...][None]
    pl.semaphore_wait(barrier, n_dev - 1)

    def g_copy(i, kind):
        t = lax.rem(c + i, nc)
        slots = gv_slots if kind == 0 else go_slots
        return remote(slots.at[c], slots.at[c], g_send.at[kind, i], g_recv.at[kind, i], r, t)

    def g_begin(kind):
        def g_start(i, _):
            g_copy(i, kind).start()
            return 0
        lax.fori_loop(1, nc, g_start, 0)

    def assemble(kind, slots, mask, store):
        def g_wait(i, _):
            g_copy(i, kind).wait_recv()
            return 0
        lax.fori_loop(1, nc, g_wait, 0)
        per = BS // w
        for j in range(na):
            block = slots[j * per:(j + 1) * per].reshape(BS, n)
            for i in range(na):
                m = mask[i, j].astype(jnp.float32)
                piece = block[:, i * BS:(i + 1) * BS].astype(jnp.float32) * m
                store(i * BS, j, piece.astype(jnp.bfloat16).T)

    def gv_store(first, j, piece):
        gv[j // 2, first:first + BS, (j % 2) * BS:(j % 2 + 1) * BS] = piece

    def go_store(first, j, piece):
        go[first:first + BS, j * BS:(j + 1) * BS] = piece

    g_begin(0)
    fetch.wait()
    for p in range(np_):
        row = jnp.concatenate(
            [jnp.full((1, BS), ri_ref[r, j, p].astype(jnp.float32)) for j in range(na)], axis=1)
        b_ref[p] = (b_ref[p].astype(jnp.float32) * row).astype(jnp.bfloat16)
    assemble(0, gv_slots, vm_ref, gv_store)
    g_begin(1)

    def round_rows(dst, s):
        def one(i, _):
            dst[s, pl.ds(i * pc, pc)] = wide[s, pl.ds(i * pc, pc)].astype(jnp.bfloat16)
            return 0
        lax.fori_loop(0, nc, one, 0)

    halves = na // 2
    group = 4

    def v_copy(s, tc):
        return remote(v16.at[s, pl.ds(tc * pc, pc)], vir_all.at[r, :, c],
                      v_send.at[s, tc], v_recv.at[r, c], s, tc)

    for t in range(halves):
        half = lax.rem(r // 2 + 1 + t, halves)
        for g in range(np_ // group):
            lhs = b_ref[g * group:(g + 1) * group].reshape(group * rows, n)
            res = jnp.dot(lhs, gv[half], preferred_element_type=jnp.float32)
            for k in range(group):
                for e in range(2):
                    wide[2 * half + e, :, g * group + k, :] = res[
                        k * rows:(k + 1) * rows, e * BS:(e + 1) * BS]
        for e in range(2):
            s = 2 * half + e
            round_rows(v16, s)
            first = (s == r).astype(jnp.int32)

            def v_start(i, _):
                v_copy(s, lax.rem(c + i, nc)).start()
                return 0

            lax.fori_loop(first, nc, v_start, 0)
    vir_all[pl.ds(r, 1), :, pl.ds(c, 1)] = v16[pl.ds(r, 1), pl.ds(c * pc, pc)][:, :, None]

    assemble(1, go_slots, om_ref, go_store)
    for g in range(np_ // 2):
        rhs = b_ref[2 * g:2 * g + 2].reshape(2 * rows, n)
        res = lax.dot_general(go[...], rhs, (((1,), (1,)), ((), ())),
                              preferred_element_type=jnp.float32)
        for k in range(2):
            for s in range(nr):
                wide[s, :, 2 * g + k, :] = res[s * BS:(s + 1) * BS, k * BS:(k + 1) * BS]
    for s in range(nr):
        round_rows(o16, s)

    def o_copy(i):
        t = lax.rem(c + i, nc)
        return remote(o16.at[:, pl.ds(t * pc, pc)], occ_all.at[:, :, c],
                      o_send.at[i], o_recv.at[i], r, t)

    def o_start(i, _):
        o_copy(i).start()
        return 0

    lax.fori_loop(1, nc, o_start, 0)
    occ_all[:, :, pl.ds(c, 1)] = o16[:, pl.ds(c * pc, pc)][:, :, None]

    def o_wait(i, _):
        o_copy(i).wait_recv()
        return 0

    lax.fori_loop(1, nc, o_wait, 0)

    total_ri = nc * np_
    chi[...] = jnp.zeros_like(chi)
    step = min(pc, 8)
    for off in range(nr):
        rr = lax.rem(r + off, nr)

        def v_wait(j, _):
            col = lax.rem(c + j, nc)
            remote(v16.at[0, pl.ds(0, pc)], vir_all.at[rr, :, col],
                   v_send.at[0, 0], v_recv.at[rr, col], rr, col).wait_recv()
            return 0

        lax.fori_loop(1 if off == 0 else 0, nc, v_wait, 0)
        for k in range(0, pc, step):
            left = occ_all[rr, k:k + step].reshape(step, total_ri, BS)
            right = vir_all[rr, k:k + step].reshape(step, total_ri, BS)
            left = jnp.concatenate([left[i] for i in range(step)], axis=1)
            right = jnp.concatenate([right[i] for i in range(step)], axis=1)
            chi[...] += lax.dot_general(
                left, right, (((1,), (1,)), ((), ())),
                preferred_element_type=jnp.float32).reshape(nc, np_, total_ri)

    def r1_copy(i):
        t = lax.rem(c + i, nc)
        return remote(chi.at[t], red1.at[c], r1_send.at[i], r1_recv.at[i], r, t)

    def r1_start(i, _):
        r1_copy(i).start()
        return 0

    lax.fori_loop(1, nc, r1_start, 0)
    red1[pl.ds(c, 1)] = chi[pl.ds(c, 1)]

    def r1_wait(i, _):
        r1_copy(i).wait_recv()
        return 0

    lax.fori_loop(1, nc, r1_wait, 0)
    part = red1[0]
    for k in range(1, nc):
        part = part + red1[k]
    wc = total_ri // nr
    for s in range(nr):
        st2[s] = part[:, s * wc:(s + 1) * wc]

    def r2_copy(i):
        t = lax.rem(r + i, nr)
        return remote(st2.at[t], red2.at[r], r2_send.at[i], r2_recv.at[i], t, c)

    for i in range(1, nr):
        r2_copy(i).start()
    red2[pl.ds(r, 1)] = st2[pl.ds(r, 1)]
    for i in range(1, nr):
        r2_copy(i).wait_recv()
    acc = red2[0]
    for k in range(1, nr):
        acc = acc + red2[k]
    out_ref[...] = acc

    for kind in (0, 1):
        def g_sent(i, _):
            g_copy(i, kind).wait_send()
            return 0
        lax.fori_loop(1, nc, g_sent, 0)

    def v_sent(i, _):
        t = lax.rem(me + i, n_dev)
        v_copy(t // nc, lax.rem(t, nc)).wait_send()
        return 0

    lax.fori_loop(1, n_dev, v_sent, 0)

    def col_sent(i, _):
        o_copy(i).wait_send()
        r1_copy(i).wait_send()
        return 0

    lax.fori_loop(1, nc, col_sent, 0)
    for i in range(1, nr):
        r2_copy(i).wait_send()


def body(nr, nc, b_tensor, ri_pairs, g_occ, g_vir, occ_mask, vir_mask):
    np_, rows, n = b_tensor.shape
    w = n // nc
    pc = rows // nc
    total_ri = nc * np_

    vmem = pl.BlockSpec(memory_space=pltpu.VMEM)
    smem = pl.BlockSpec(memory_space=pltpu.SMEM)
    bf16, f32 = jnp.bfloat16, jnp.float32
    dma = pltpu.SemaphoreType.DMA
    return pl.pallas_call(
        functools.partial(kernel, nr, nc),
        out_shape=jax.ShapeDtypeStruct((np_, total_ri // nr), f32),
        in_specs=[smem, smem, smem, pl.BlockSpec(memory_space=pl.ANY), vmem, vmem],
        out_specs=vmem,
        scratch_shapes=[
            pltpu.VMEM((np_, rows, n), bf16),
            pltpu.VMEM((nc, w, n), bf16),
            pltpu.VMEM((nc, w, n), bf16),
            pltpu.VMEM((n // (2 * BS), n, 2 * BS), bf16),
            pltpu.VMEM((n, n), bf16),
            pltpu.VMEM((nr, rows, np_, BS), f32),
            pltpu.VMEM((nr, rows, np_, BS), bf16),
            pltpu.VMEM((nr, rows, np_, BS), bf16),
            pltpu.VMEM((nr, pc, nc, np_, BS), bf16),
            pltpu.VMEM((nr, pc, nc, np_, BS), bf16),
            pltpu.VMEM((nc, np_, total_ri), f32),
            pltpu.VMEM((nc, np_, total_ri), f32),
            pltpu.VMEM((nr, np_, total_ri // nr), f32),
            pltpu.VMEM((nr, np_, total_ri // nr), f32),
            dma, dma((2, nc)), dma((2, nc)),
            dma((nr, nc)), dma((nr, nc)),
            dma((nc,)), dma((nc,)),
            dma((nc,)), dma((nc,)),
            dma((nr,)), dma((nr,)),
        ],
        compiler_params=pltpu.CompilerParams(
            collective_id=0, has_side_effects=True, vmem_limit_bytes=56 * 1024 * 1024),
    )(ri_pairs.transpose(1, 2, 0), occ_mask, vir_mask, b_tensor, g_occ.T, g_vir.T)


def solution(mesh):
    in_specs = (
        P("col", "row", None),
        P("col", None, None),
        P(None, "col"),
        P(None, "col"),
        P(),
        P(),
    )
    return jax.shard_map(
        functools.partial(body, mesh.shape["row"], mesh.shape["col"]),
        mesh=mesh, in_specs=in_specs, out_specs=P("col", "row"), check_vma=False)
```

```python
import functools

import jax
import jax.numpy as jnp
from jax import lax
from jax.experimental import pallas as pl
from jax.experimental.pallas import tpu as pltpu
from jax.sharding import PartitionSpec as P

BS = 128


def kernel(nr, nc, ri_ref, om_ref, vm_ref, b_hbm, go_ref, gv_ref, out_ref,
           b_ref, gv_slots, go_slots, gv, go, wide, v16, o16, vir_all, occ_all,
           chi, red1, st2, red2,
           b_sem, g_send, g_recv, v_send, v_recv, o_send, o_recv,
           r1_send, r1_recv, r2_send, r2_recv):
    r = lax.axis_index("row")
    c = lax.axis_index("col")
    me = r * nc + c
    n_dev = nr * nc
    np_, rows, n = b_ref.shape
    na = n // BS
    pc = rows // nc
    w = n // nc

    def remote(src, dst, send, recv, row, col):
        return pltpu.make_async_remote_copy(
            src_ref=src, dst_ref=dst, send_sem=send, recv_sem=recv,
            device_id={"row": row, "col": col}, device_id_type=pl.DeviceIdType.MESH)

    fetch = pltpu.make_async_copy(b_hbm, b_ref, b_sem)
    fetch.start()
    barrier = pltpu.get_barrier_semaphore()

    def greet(i, _):
        t = lax.rem(me + i, n_dev)
        pl.semaphore_signal(barrier, inc=1,
                            device_id={"row": t // nc, "col": lax.rem(t, nc)},
                            device_id_type=pl.DeviceIdType.MESH)
        return 0

    lax.fori_loop(1, n_dev, greet, 0)
    for src, slots in ((gv_ref, gv_slots), (go_ref, go_slots)):
        slots[pl.ds(c, 1)] = src[...][None]
    pl.semaphore_wait(barrier, n_dev - 1)

    def g_copy(i, kind):
        t = lax.rem(c + i, nc)
        slots = gv_slots if kind == 0 else go_slots
        return remote(slots.at[c], slots.at[c], g_send.at[kind, i], g_recv.at[kind, i], r, t)

    def g_begin(kind):
        def g_start(i, _):
            g_copy(i, kind).start()
            return 0
        lax.fori_loop(1, nc, g_start, 0)

    per = BS // w
    shards = 2 * per

    def arrived(kind, half=None):
        def g_wait(i, _):
            if half is None:
                g_copy(i, kind).wait_recv()
            else:
                @pl.when(lax.rem(c + nc - i, nc) // shards == half)
                def _():
                    g_copy(i, kind).wait_recv()
            return 0
        lax.fori_loop(1, nc, g_wait, 0)

    def assemble(slots, mask, j, store):
        block = slots[pl.ds(j * per, per)].reshape(BS, n)
        for i in range(na):
            m = mask[i, j].astype(jnp.float32)
            piece = block[:, i * BS:(i + 1) * BS].astype(jnp.float32) * m
            store(i * BS, j, piece.astype(jnp.bfloat16).T)

    def go_store(first, j, piece):
        go[first:first + BS, j * BS:(j + 1) * BS] = piece

    halves = na // 2
    far = lax.rem(r // 2 + 1, halves)

    @pl.when(c // shards == far)
    def _():
        g_begin(0)

    fetch.wait()
    for p in range(np_):
        row = jnp.concatenate(
            [jnp.full((1, BS), ri_ref[r, j, p].astype(jnp.float32)) for j in range(na)], axis=1)
        b_ref[p] = (b_ref[p].astype(jnp.float32) * row).astype(jnp.bfloat16)

    def round_rows(dst, s):
        def one(i, _):
            dst[s, pl.ds(i * pc, pc)] = wide[s, pl.ds(i * pc, pc)].astype(jnp.bfloat16)
            return 0
        lax.fori_loop(0, nc, one, 0)

    group = 4

    def v_copy(s, tc):
        return remote(v16.at[s, pl.ds(tc * pc, pc)], vir_all.at[r, c],
                      v_send.at[s, tc], v_recv.at[r, c], s, tc)

    for t in range(halves):
        half = lax.rem(far + t, halves)
        arrived(0, half)
        for e in range(2):
            def gv_store(first, j, piece, e=e):
                gv[half, first:first + BS, e * BS:(e + 1) * BS] = piece

            assemble(gv_slots, vm_ref, 2 * half + e, gv_store)
        if t == 0:
            @pl.when(c // shards != far)
            def _():
                g_begin(0)

            g_begin(1)
        for g in range(np_ // group):
            lhs = b_ref[g * group:(g + 1) * group].reshape(group * rows, n)
            res = jnp.dot(lhs, gv[half], preferred_element_type=jnp.float32)
            for k in range(group):
                for e in range(2):
                    wide[2 * half + e, :, g * group + k, :] = res[
                        k * rows:(k + 1) * rows, e * BS:(e + 1) * BS]
        for e in range(2):
            s = 2 * half + jnp.where(half > r // 2, 1 - e, e)
            round_rows(v16, s)
            first = (s == r).astype(jnp.int32)

            def v_start(i, _):
                v_copy(s, lax.rem(c + i, nc)).start()
                return 0

            lax.fori_loop(first, nc, v_start, 0)
    vir_all[pl.ds(r, 1), pl.ds(c, 1)] = v16[pl.ds(r, 1), pl.ds(c * pc, pc)][:, None]

    arrived(1)
    for j in range(na):
        assemble(go_slots, om_ref, j, go_store)
    for g in range(np_ // 2):
        rhs = b_ref[2 * g:2 * g + 2].reshape(2 * rows, n)
        res = lax.dot_general(go[...], rhs, (((1,), (1,)), ((), ())),
                              preferred_element_type=jnp.float32)
        for k in range(2):
            for s in range(nr):
                wide[s, :, 2 * g + k, :] = res[s * BS:(s + 1) * BS, k * BS:(k + 1) * BS]
    for s in range(nr):
        round_rows(o16, s)

    def o_copy(i):
        t = lax.rem(c + i, nc)
        return remote(o16.at[:, pl.ds(t * pc, pc)], occ_all.at[:, c],
                      o_send.at[i], o_recv.at[i], r, t)

    def o_start(i, _):
        o_copy(i).start()
        return 0

    lax.fori_loop(1, nc, o_start, 0)
    occ_all[:, pl.ds(c, 1)] = o16[:, pl.ds(c * pc, pc)][:, None]

    def o_wait(i, _):
        o_copy(i).wait_recv()
        return 0

    lax.fori_loop(1, nc, o_wait, 0)

    total_ri = nc * np_
    chi[...] = jnp.zeros_like(chi)
    step = min(pc, 8)
    for off in range(nr):
        rr = lax.rem(r + off, nr)

        def v_wait(j, _):
            col = lax.rem(c + j, nc)
            remote(v16.at[0, pl.ds(0, pc)], vir_all.at[rr, col],
                   v_send.at[0, 0], v_recv.at[rr, col], rr, col).wait_recv()
            return 0

        lax.fori_loop(1 if off == 0 else 0, nc, v_wait, 0)
        for k in range(0, pc, step):
            left, right = (
                jnp.concatenate([full[rr, :, k + i].reshape(total_ri, BS) for i in range(step)], axis=1)
                for full in (occ_all, vir_all))
            chi[...] += lax.dot_general(
                left, right, (((1,), (1,)), ((), ())),
                preferred_element_type=jnp.float32).reshape(nc, np_, total_ri)

    def r1_copy(i):
        t = lax.rem(c + i, nc)
        return remote(chi.at[t], red1.at[c], r1_send.at[i], r1_recv.at[i], r, t)

    def r1_start(i, _):
        r1_copy(i).start()
        return 0

    lax.fori_loop(1, nc, r1_start, 0)
    red1[pl.ds(c, 1)] = chi[pl.ds(c, 1)]

    def r1_wait(i, _):
        r1_copy(i).wait_recv()
        return 0

    lax.fori_loop(1, nc, r1_wait, 0)
    part = red1[0]
    for k in range(1, nc):
        part = part + red1[k]
    wc = total_ri // nr
    for s in range(nr):
        st2[s] = part[:, s * wc:(s + 1) * wc]

    def r2_copy(i):
        t = lax.rem(r + i, nr)
        return remote(st2.at[t], red2.at[r], r2_send.at[i], r2_recv.at[i], t, c)

    for i in range(1, nr):
        r2_copy(i).start()
    red2[pl.ds(r, 1)] = st2[pl.ds(r, 1)]
    for i in range(1, nr):
        r2_copy(i).wait_recv()
    acc = red2[0]
    for k in range(1, nr):
        acc = acc + red2[k]
    out_ref[...] = acc

    for kind in (0, 1):
        def g_sent(i, _):
            g_copy(i, kind).wait_send()
            return 0
        lax.fori_loop(1, nc, g_sent, 0)

    def v_sent(i, _):
        t = lax.rem(me + i, n_dev)
        v_copy(t // nc, lax.rem(t, nc)).wait_send()
        return 0

    lax.fori_loop(1, n_dev, v_sent, 0)

    def col_sent(i, _):
        o_copy(i).wait_send()
        r1_copy(i).wait_send()
        return 0

    lax.fori_loop(1, nc, col_sent, 0)
    for i in range(1, nr):
        r2_copy(i).wait_send()


def body(nr, nc, b_tensor, ri_pairs, g_occ, g_vir, occ_mask, vir_mask):
    np_, rows, n = b_tensor.shape
    w = n // nc
    pc = rows // nc
    total_ri = nc * np_

    vmem = pl.BlockSpec(memory_space=pltpu.VMEM)
    smem = pl.BlockSpec(memory_space=pltpu.SMEM)
    bf16, f32 = jnp.bfloat16, jnp.float32
    dma = pltpu.SemaphoreType.DMA
    return pl.pallas_call(
        functools.partial(kernel, nr, nc),
        out_shape=jax.ShapeDtypeStruct((np_, total_ri // nr), f32),
        in_specs=[smem, smem, smem, pl.BlockSpec(memory_space=pl.ANY), vmem, vmem],
        out_specs=vmem,
        scratch_shapes=[
            pltpu.VMEM((np_, rows, n), bf16),
            pltpu.VMEM((nc, w, n), bf16),
            pltpu.VMEM((nc, w, n), bf16),
            pltpu.VMEM((n // (2 * BS), n, 2 * BS), bf16),
            pltpu.VMEM((n, n), bf16),
            pltpu.VMEM((nr, rows, np_, BS), f32),
            pltpu.VMEM((nr, rows, np_, BS), bf16),
            pltpu.VMEM((nr, rows, np_, BS), bf16),
            pltpu.VMEM((nr, nc, pc, np_, BS), bf16),
            pltpu.VMEM((nr, nc, pc, np_, BS), bf16),
            pltpu.VMEM((nc, np_, total_ri), f32),
            pltpu.VMEM((nc, np_, total_ri), f32),
            pltpu.VMEM((nr, np_, total_ri // nr), f32),
            pltpu.VMEM((nr, np_, total_ri // nr), f32),
            dma, dma((2, nc)), dma((2, nc)),
            dma((nr, nc)), dma((nr, nc)),
            dma((nc,)), dma((nc,)),
            dma((nc,)), dma((nc,)),
            dma((nr,)), dma((nr,)),
        ],
        compiler_params=pltpu.CompilerParams(
            collective_id=0, has_side_effects=True, vmem_limit_bytes=56 * 1024 * 1024),
    )(ri_pairs.transpose(1, 2, 0), occ_mask, vir_mask, b_tensor, g_occ.T, g_vir.T)


def solution(mesh):
    in_specs = (
        P("col", "row", None),
        P("col", None, None),
        P(None, "col"),
        P(None, "col"),
        P(),
        P(),
    )
    return jax.shard_map(
        functools.partial(body, mesh.shape["row"], mesh.shape["col"]),
        mesh=mesh, in_specs=in_specs, out_specs=P("col", "row"), check_vma=False)
```

```python
import functools

import jax
import jax.numpy as jnp
from jax import lax
from jax.experimental import pallas as pl
from jax.experimental.pallas import tpu as pltpu
from jax.sharding import PartitionSpec as P

BS = 128


def kernel(nr, nc, ri_ref, om_ref, vm_ref, b_hbm, go_ref, gv_ref, out_ref,
           b_ref, gv_slots, go_slots, gv, go, wide, v16, o16, vir_all, occ_all,
           chi, red1, st2, red2,
           b_sem, g_send, g_recv, v_send, v_recv, o_send, o_recv,
           r1_send, r1_recv, r2_send, r2_recv):
    r = lax.axis_index("row")
    c = lax.axis_index("col")
    me = r * nc + c
    n_dev = nr * nc
    np_, rows, n = b_ref.shape
    na = n // BS
    pc = rows // nc
    w = n // nc

    def remote(src, dst, send, recv, row, col):
        return pltpu.make_async_remote_copy(
            src_ref=src, dst_ref=dst, send_sem=send, recv_sem=recv,
            device_id={"row": row, "col": col}, device_id_type=pl.DeviceIdType.MESH)

    fetch = pltpu.make_async_copy(b_hbm, b_ref, b_sem)
    fetch.start()
    barrier = pltpu.get_barrier_semaphore()

    def greet(i, _):
        t = lax.rem(me + i, n_dev)
        pl.semaphore_signal(barrier, inc=1,
                            device_id={"row": t // nc, "col": lax.rem(t, nc)},
                            device_id_type=pl.DeviceIdType.MESH)
        return 0

    lax.fori_loop(1, n_dev, greet, 0)
    for src, slots in ((gv_ref, gv_slots), (go_ref, go_slots)):
        slots[pl.ds(c, 1)] = src[...][None]
    pl.semaphore_wait(barrier, n_dev - 1)

    def g_copy(i, kind):
        t = lax.rem(c + i, nc)
        slots = gv_slots if kind == 0 else go_slots
        return remote(slots.at[c], slots.at[c], g_send.at[kind, i], g_recv.at[kind, i], r, t)

    def g_begin(kind):
        def g_start(i, _):
            g_copy(i, kind).start()
            return 0
        lax.fori_loop(1, nc, g_start, 0)

    def assemble(kind, slots, mask, store):
        def g_wait(i, _):
            g_copy(i, kind).wait_recv()
            return 0
        lax.fori_loop(1, nc, g_wait, 0)
        per = BS // w
        for j in range(na):
            block = slots[j * per:(j + 1) * per].reshape(BS, n)
            for i in range(na):
                m = mask[i, j].astype(jnp.float32)
                piece = block[:, i * BS:(i + 1) * BS].astype(jnp.float32) * m
                store(i * BS, j, piece.astype(jnp.bfloat16).T)

    def gv_store(first, j, piece):
        gv[j // 2, first:first + BS, (j % 2) * BS:(j % 2 + 1) * BS] = piece

    def go_store(first, j, piece):
        go[first:first + BS, j * BS:(j + 1) * BS] = piece

    g_begin(0)
    fetch.wait()
    for p in range(np_):
        row = jnp.concatenate(
            [jnp.full((1, BS), ri_ref[r, j, p].astype(jnp.float32)) for j in range(na)], axis=1)
        b_ref[p] = (b_ref[p].astype(jnp.float32) * row).astype(jnp.bfloat16)
    assemble(0, gv_slots, vm_ref, gv_store)
    g_begin(1)

    def round_rows(dst, s):
        def one(i, _):
            dst[s, pl.ds(i * pc, pc)] = wide[s, pl.ds(i * pc, pc)].astype(jnp.bfloat16)
            return 0
        lax.fori_loop(0, nc, one, 0)

    halves = na // 2
    group = 4

    def v_copy(s, tc):
        return remote(v16.at[s, pl.ds(tc * pc, pc)], vir_all.at[r, c],
                      v_send.at[s, tc], v_recv.at[r, c], s, tc)

    for t in range(halves):
        half = lax.rem(r // 2 + 1 + t, halves)
        for g in range(np_ // group):
            lhs = b_ref[g * group:(g + 1) * group].reshape(group * rows, n)
            res = jnp.dot(lhs, gv[half], preferred_element_type=jnp.float32)
            for k in range(group):
                for e in range(2):
                    wide[2 * half + e, :, g * group + k, :] = res[
                        k * rows:(k + 1) * rows, e * BS:(e + 1) * BS]
        for e in range(2):
            s = 2 * half + e
            round_rows(v16, s)
            first = (s == r).astype(jnp.int32)

            def v_start(i, _):
                v_copy(s, lax.rem(c + i, nc)).start()
                return 0

            lax.fori_loop(first, nc, v_start, 0)
    vir_all[pl.ds(r, 1), pl.ds(c, 1)] = v16[pl.ds(r, 1), pl.ds(c * pc, pc)][:, None]

    assemble(1, go_slots, om_ref, go_store)
    for g in range(np_ // 2):
        rhs = b_ref[2 * g:2 * g + 2].reshape(2 * rows, n)
        res = lax.dot_general(go[...], rhs, (((1,), (1,)), ((), ())),
                              preferred_element_type=jnp.float32)
        for k in range(2):
            for s in range(nr):
                wide[s, :, 2 * g + k, :] = res[s * BS:(s + 1) * BS, k * BS:(k + 1) * BS]
    for s in range(nr):
        round_rows(o16, s)

    def o_copy(i):
        t = lax.rem(c + i, nc)
        return remote(o16.at[:, pl.ds(t * pc, pc)], occ_all.at[:, c],
                      o_send.at[i], o_recv.at[i], r, t)

    def o_start(i, _):
        o_copy(i).start()
        return 0

    lax.fori_loop(1, nc, o_start, 0)
    occ_all[:, pl.ds(c, 1)] = o16[:, pl.ds(c * pc, pc)][:, None]

    def o_wait(i, _):
        o_copy(i).wait_recv()
        return 0

    lax.fori_loop(1, nc, o_wait, 0)

    total_ri = nc * np_
    chi[...] = jnp.zeros_like(chi)
    step = min(pc, 8)
    for off in range(nr):
        rr = lax.rem(r + off, nr)

        def v_wait(j, _):
            col = lax.rem(c + j, nc)
            remote(v16.at[0, pl.ds(0, pc)], vir_all.at[rr, col],
                   v_send.at[0, 0], v_recv.at[rr, col], rr, col).wait_recv()
            return 0

        lax.fori_loop(1 if off == 0 else 0, nc, v_wait, 0)
        for k in range(0, pc, step):
            left, right = (
                jnp.concatenate([full[rr, :, k + i].reshape(total_ri, BS) for i in range(step)], axis=1)
                for full in (occ_all, vir_all))
            chi[...] += lax.dot_general(
                left, right, (((1,), (1,)), ((), ())),
                preferred_element_type=jnp.float32).reshape(nc, np_, total_ri)

    def r1_copy(i):
        t = lax.rem(c + i, nc)
        return remote(chi.at[t], red1.at[c], r1_send.at[i], r1_recv.at[i], r, t)

    def r1_start(i, _):
        r1_copy(i).start()
        return 0

    lax.fori_loop(1, nc, r1_start, 0)
    red1[pl.ds(c, 1)] = chi[pl.ds(c, 1)]

    def r1_wait(i, _):
        r1_copy(i).wait_recv()
        return 0

    lax.fori_loop(1, nc, r1_wait, 0)
    part = red1[0]
    for k in range(1, nc):
        part = part + red1[k]
    wc = total_ri // nr
    for s in range(nr):
        st2[s] = part[:, s * wc:(s + 1) * wc]

    def r2_copy(i):
        t = lax.rem(r + i, nr)
        return remote(st2.at[t], red2.at[r], r2_send.at[i], r2_recv.at[i], t, c)

    for i in range(1, nr):
        r2_copy(i).start()
    red2[pl.ds(r, 1)] = st2[pl.ds(r, 1)]
    for i in range(1, nr):
        r2_copy(i).wait_recv()
    acc = red2[0]
    for k in range(1, nr):
        acc = acc + red2[k]
    out_ref[...] = acc

    for kind in (0, 1):
        def g_sent(i, _):
            g_copy(i, kind).wait_send()
            return 0
        lax.fori_loop(1, nc, g_sent, 0)

    def v_sent(i, _):
        t = lax.rem(me + i, n_dev)
        v_copy(t // nc, lax.rem(t, nc)).wait_send()
        return 0

    lax.fori_loop(1, n_dev, v_sent, 0)

    def col_sent(i, _):
        o_copy(i).wait_send()
        r1_copy(i).wait_send()
        return 0

    lax.fori_loop(1, nc, col_sent, 0)
    for i in range(1, nr):
        r2_copy(i).wait_send()


def body(nr, nc, b_tensor, ri_pairs, g_occ, g_vir, occ_mask, vir_mask):
    np_, rows, n = b_tensor.shape
    w = n // nc
    pc = rows // nc
    total_ri = nc * np_

    vmem = pl.BlockSpec(memory_space=pltpu.VMEM)
    smem = pl.BlockSpec(memory_space=pltpu.SMEM)
    bf16, f32 = jnp.bfloat16, jnp.float32
    dma = pltpu.SemaphoreType.DMA
    return pl.pallas_call(
        functools.partial(kernel, nr, nc),
        out_shape=jax.ShapeDtypeStruct((np_, total_ri // nr), f32),
        in_specs=[smem, smem, smem, pl.BlockSpec(memory_space=pl.ANY), vmem, vmem],
        out_specs=vmem,
        scratch_shapes=[
            pltpu.VMEM((np_, rows, n), bf16),
            pltpu.VMEM((nc, w, n), bf16),
            pltpu.VMEM((nc, w, n), bf16),
            pltpu.VMEM((n // (2 * BS), n, 2 * BS), bf16),
            pltpu.VMEM((n, n), bf16),
            pltpu.VMEM((nr, rows, np_, BS), f32),
            pltpu.VMEM((nr, rows, np_, BS), bf16),
            pltpu.VMEM((nr, rows, np_, BS), bf16),
            pltpu.VMEM((nr, nc, pc, np_, BS), bf16),
            pltpu.VMEM((nr, nc, pc, np_, BS), bf16),
            pltpu.VMEM((nc, np_, total_ri), f32),
            pltpu.VMEM((nc, np_, total_ri), f32),
            pltpu.VMEM((nr, np_, total_ri // nr), f32),
            pltpu.VMEM((nr, np_, total_ri // nr), f32),
            dma, dma((2, nc)), dma((2, nc)),
            dma((nr, nc)), dma((nr, nc)),
            dma((nc,)), dma((nc,)),
            dma((nc,)), dma((nc,)),
            dma((nr,)), dma((nr,)),
        ],
        compiler_params=pltpu.CompilerParams(
            collective_id=0, has_side_effects=True, vmem_limit_bytes=56 * 1024 * 1024),
    )(ri_pairs.transpose(1, 2, 0), occ_mask, vir_mask, b_tensor, g_occ.T, g_vir.T)


def solution(mesh):
    in_specs = (
        P("col", "row", None),
        P("col", None, None),
        P(None, "col"),
        P(None, "col"),
        P(),
        P(),
    )
    return jax.shard_map(
        functools.partial(body, mesh.shape["row"], mesh.shape["col"]),
        mesh=mesh, in_specs=in_specs, out_specs=P("col", "row"), check_vma=False)
```
